512 devices in a mesh: fsdp: 32 (over y, z_hi, x), tensor: 16 (over z_lo, core).
Axes of the slice: x: 4, y: 4, z: 16 (z_hi: 2, z_lo: 8; z = z_hi * 8 + z_lo), core: 2. Of those that a mesh axis runs over, the one named last changes fastest.
Arguments:
- tokens: bfloat16 [512, 9216], P(None, 'tensor'), may hold values from -800 to 800
- ln_gain: bfloat16 [9216], P('tensor'), may hold values from 0.099609375 to 1.8984375
- ln_bias: bfloat16 [9216], P('tensor'), may hold values from -3 to 3
- fc1_weight: bfloat16 [9216, 36864], P('tensor', 'fsdp'), may hold values from -0.0625 to 0.0625
- fc1_bias: bfloat16 [36864], P('fsdp'), may hold values from -3 to 3
- fc2_weight: bfloat16 [36864, 9216], P('fsdp', 'tensor'), may hold values from -0.03125 to 0.03125
- fc2_bias: bfloat16 [9216], P('tensor'), may hold values from -3 to 3
- update_step: float32 [1], replicated, may hold values from -0.004 to 0.004
- perturb_scale: float32 [1], replicated, may hold values from 0.002 to 0.008
- step_seeds: int32 [2], replicated, may hold values from 0 to 16777215
- hash_mults: int32 [3], replicated, may hold values from 65537 to 16777215
Outputs:
- branch_plus: bfloat16 [512, 9216], P('fsdp', 'tensor')
- branch_minus: bfloat16 [512, 9216], P('fsdp', 'tensor')
The draws below stay inside these ranges and needn't reach their ends.
Inputs may be any that keep to these rules, and one draw needn't show every extreme that they name: `step_seeds`: the previous step's seed, then this step's. `hash_mults`: three multipliers; the lowest bit is set before use.
All inputs are finite; a program needn't handle non-finite values.
Results may differ from the reference program's by a relative error of at most 0.03.
Values may be sent and summed in bfloat16 or wider, within the bound.
No kernel may reach another device: no remote copies, remote signals or barrier semaphores. Data moves between devices by JAX's collectives and lax.ppermute only.
A program may use at most 64 MiB of HBM per device.

```python
import math
import jax
import jax.numpy as jnp
from jax import lax

D = 9216
FF = 36864
TOK = 512
N_FSDP = 32
N_TENSOR = 16


def draw_tokens(key, part):
    key_base = jax.random.fold_in(key, 0)
    key_offset = jax.random.fold_in(key, 1)
    key_rows = jax.random.fold_in(key, 2)
    key_coarse = jax.random.fold_in(key, 4)
    key_fine = jax.random.fold_in(key, 5)
    coarse_level = jax.random.uniform(key_coarse, (16,), jnp.float32, 0.0, 0.9)
    coarse_cols = jnp.repeat(coarse_level, D // 16)
    fine_level = jax.random.uniform(key_fine, (D,), jnp.float32, 0.0, 0.3)
    column_scale = jnp.power(10.0, coarse_cols + fine_level)[None, :]
    row_scale = jnp.power(10.0, jax.random.uniform(key_rows, (TOK, 1), jnp.float32))
    spread_offset = jnp.clip(jax.random.normal(key_offset, (1, D), jnp.float32), -2.0, 2.0) * 0.5
    base_vals = jnp.clip(jax.random.normal(key_base, (TOK, D), jnp.float32), -3.0, 3.0)
    column_offset = 1.0 + spread_offset
    return ((base_vals + column_offset) * column_scale * row_scale).astype(jnp.bfloat16)


def block_levels(rng, extent, shards, least, high):
    factor_of, own = 1.0, jax.random.fold_in(rng, 6)
    for position, shards_of in shards:
        draws = jnp.exp(jax.random.uniform(jax.random.fold_in(own, position), (shards_of,), jnp.float32, least / len(shards), high / len(shards)))
        factor_of = factor_of * jnp.repeat(draws, extent[position] // shards_of).reshape([-1 if axis == position else 1 for axis in range(len(extent))])
    return factor_of


def bell_draw(rng, extent, deviation, limit, cuts=(), kind=jnp.bfloat16):
    gain = block_levels(rng, extent, cuts, -0.22, 0.18) if cuts else 1.0
    values = jax.random.normal(rng, extent, jnp.float32) * deviation * gain
    return jnp.minimum(jnp.maximum(values, -limit), limit).astype(kind)


def setup_inputs(seed: int = 0) -> dict:
    key_of = jax.random.split(jax.random.key(seed), 12)
    tokens = draw_tokens(jax.random.fold_in(key_of[11], 71), 0)
    ln_gain = jnp.clip(1.0 + 0.18 * jax.random.normal(key_of[1], (D,), jnp.float32), 0.099609375, 1.8984375).astype(jnp.bfloat16)
    ln_bias = bell_draw(key_of[2], (D,), 0.5, 3.0, ((0, 16),))
    fc1_weight = bell_draw(key_of[3], (D, FF), D ** -0.5, 0.0625, ((0, 16), (1, 32)))
    fc1_bias = bell_draw(key_of[4], (FF,), 0.5, 3.0, ((0, 32),))
    fc2_weight = bell_draw(key_of[5], (FF, D), FF ** -0.5, 0.03125, ((0, 32), (1, 16)))
    fc2_bias = bell_draw(key_of[6], (D,), 0.5, 3.0, ((0, 16),))
    update_step = jnp.clip(jax.random.uniform(key_of[7], (1,), jnp.float32, -0.004, 0.004), -0.004, 0.004)
    perturb_scale = jnp.clip(jnp.exp(jax.random.uniform(key_of[8], (1,), jnp.float32, math.log(0.002), math.log(0.008))), 0.002, 0.008)
    step_seeds = jax.random.randint(key_of[9], (2,), 0, 16777216).astype(jnp.int32)
    hash_mults = jax.random.randint(key_of[10], (3,), 65537, 16777216).astype(jnp.int32)
    return dict(tokens=tokens, ln_gain=ln_gain, ln_bias=ln_bias, fc1_weight=fc1_weight, fc1_bias=fc1_bias, fc2_weight=fc2_weight, fc2_bias=fc2_bias, update_step=update_step, perturb_scale=perturb_scale, step_seeds=step_seeds, hash_mults=hash_mults)


def shift_xor(hashed, amount):
    return hashed ^ lax.shift_right_logical(hashed, jnp.int32(amount))

def hashed_noise(param_index, seed_value, hash_mults):
    mult_a = hash_mults[0] | 1
    mult_b = hash_mults[1] | 1
    mult_c = hash_mults[2] | 1
    hashed = param_index * mult_a + seed_value * mult_b
    hashed = shift_xor(hashed, 16)
    hashed = hashed * mult_c
    hashed = shift_xor(hashed, 13)
    hashed = hashed * mult_a
    hashed = shift_xor(hashed, 16)
    fraction = (hashed & 16777215).astype(jnp.float32) * (1.0 / 16777216.0)
    return (fraction - 0.5) * 3.4641016151377544

def new_weights(weight, param_index, update_step, perturb_scale, step_seeds, hash_mults):
    updated = (weight.astype(jnp.float32) - update_step[0] * hashed_noise(param_index, step_seeds[0], hash_mults)).astype(jnp.bfloat16)
    updated = lax.optimization_barrier(updated)
    updated_f = updated.astype(jnp.float32)
    shift_term = perturb_scale[0] * hashed_noise(param_index, step_seeds[1], hash_mults)
    return ((updated_f + shift_term).astype(jnp.bfloat16), (updated_f - shift_term).astype(jnp.bfloat16))

def rounded_dot(left_side, right_side):
    product = jnp.dot(left_side, right_side, preferred_element_type=jnp.float32).astype(jnp.bfloat16)
    product = lax.optimization_barrier(product)
    return product.astype(jnp.float32)

def reference(tokens, ln_gain, ln_bias, fc1_weight, fc1_bias, fc2_weight, fc2_bias, update_step, perturb_scale, step_seeds, hash_mults):
    values = tokens.astype(jnp.float32)
    row_mean = lax.optimization_barrier(jnp.mean(values, axis=1, keepdims=True))
    centered = values - row_mean
    row_var = lax.optimization_barrier(jnp.mean(centered * centered, axis=1, keepdims=True))
    normed = (centered * lax.rsqrt(row_var + 1e-05) * ln_gain.astype(jnp.float32) + ln_bias.astype(jnp.float32)).astype(jnp.bfloat16)
    feat_block = D // N_TENSOR
    unit_block = FF // N_FSDP
    unit_all = jnp.arange(FF, dtype=jnp.int32)
    feat_all = jnp.arange(D, dtype=jnp.int32)

    def first_layer(running, block_id):
        start_row = (block_id * feat_block).astype(jnp.int32)
        row_ids = start_row + jnp.arange(feat_block, dtype=jnp.int32)
        weight = lax.dynamic_slice_in_dim(fc1_weight, start_row, feat_block, 0)
        param_index = row_ids[:, None] * FF + unit_all[None, :]
        plus_w, minus_w = new_weights(weight, param_index, update_step, perturb_scale, step_seeds, hash_mults)
        inputs = lax.dynamic_slice_in_dim(normed, start_row, feat_block, 1)
        return ((running[0] + rounded_dot(inputs, plus_w), running[1] + rounded_dot(inputs, minus_w)), None)
    zero_first = jnp.zeros((TOK, FF), jnp.float32)
    (first_plus, first_minus), _ = lax.scan(first_layer, (zero_first, zero_first), jnp.arange(N_TENSOR, dtype=jnp.int32))
    bias_one = fc1_bias.astype(jnp.float32)
    hidden_plus = jax.nn.relu(first_plus + bias_one).astype(jnp.bfloat16)
    hidden_minus = jax.nn.relu(first_minus + bias_one).astype(jnp.bfloat16)

    def second_layer(running, block_id):
        start_row = (block_id * unit_block).astype(jnp.int32)
        row_ids = start_row + jnp.arange(unit_block, dtype=jnp.int32)
        weight = lax.dynamic_slice_in_dim(fc2_weight, start_row, unit_block, 0)
        param_index = D * FF + row_ids[:, None] * D + feat_all[None, :]
        plus_w, minus_w = new_weights(weight, param_index, update_step, perturb_scale, step_seeds, hash_mults)
        slab_plus = lax.dynamic_slice_in_dim(hidden_plus, start_row, unit_block, 1)
        slab_minus = lax.dynamic_slice_in_dim(hidden_minus, start_row, unit_block, 1)
        return ((running[0] + rounded_dot(slab_plus, plus_w), running[1] + rounded_dot(slab_minus, minus_w)), None)
    zero_second = jnp.zeros((TOK, D), jnp.float32)
    (second_plus, second_minus), _ = lax.scan(second_layer, (zero_second, zero_second), jnp.arange(N_FSDP, dtype=jnp.int32))
    bias_two = fc2_bias.astype(jnp.float32)
    branch_plus = (second_plus + bias_two).astype(jnp.bfloat16)
    branch_minus = (second_minus + bias_two).astype(jnp.bfloat16)
    return (branch_plus, branch_minus)
```

```python
import jax
import jax.numpy as jnp
from jax import lax
from jax.sharding import Mesh, PartitionSpec as P

D = 9216
FF = 36864
TENSOR = ("zl", "c")
FSDP = ("y", "zh", "x")


def shift_xor(hashed, amount):
    return hashed ^ lax.shift_right_logical(hashed, jnp.int32(amount))


def hashed_noise(param_index, seed_value, hash_mults):
    mult_a = hash_mults[0] | 1
    mult_b = hash_mults[1] | 1
    mult_c = hash_mults[2] | 1
    hashed = param_index * mult_a + seed_value * mult_b
    hashed = shift_xor(hashed, 16)
    hashed = hashed * mult_c
    hashed = shift_xor(hashed, 13)
    hashed = hashed * mult_a
    hashed = shift_xor(hashed, 16)
    fraction = (hashed & 16777215).astype(jnp.float32) * (1.0 / 16777216.0)
    return (fraction - 0.5) * 3.4641016151377544


def new_weights(weight, param_index, update_step, perturb_scale, step_seeds, hash_mults):
    updated = (
        weight.astype(jnp.float32)
        - update_step[0] * hashed_noise(param_index, step_seeds[0], hash_mults)
    ).astype(jnp.bfloat16)
    updated = lax.optimization_barrier(updated)
    updated_f = updated.astype(jnp.float32)
    shift_term = perturb_scale[0] * hashed_noise(param_index, step_seeds[1], hash_mults)
    return (
        (updated_f + shift_term).astype(jnp.bfloat16),
        (updated_f - shift_term).astype(jnp.bfloat16),
    )


def line_perm(bit_of_core):
    return [(2 * z + c, 2 * (z ^ (1 << bit_of_core[c])) + c) for z in range(8) for c in range(2)]


STAGES = [(0, 1), (1, 0), (2, 2)]
CORE_SWAP = [(i, i ^ 1) for i in range(16)]


def total(value):
    value = value + lax.ppermute(value, TENSOR, CORE_SWAP)
    for bits in STAGES:
        value = value + lax.ppermute(value, TENSOR, line_perm(bits))
    return value


def half(array, which):
    rows = array.shape[0] // 2
    return lax.dynamic_slice_in_dim(array, which * rows, rows, 0)


def join(mine, other, which):
    return jnp.where(
        which == 0, jnp.concatenate([mine, other], 0), jnp.concatenate([other, mine], 0)
    )


def body(
    tokens,
    ln_gain,
    ln_bias,
    fc1_weight,
    fc1_bias,
    fc2_weight,
    fc2_bias,
    update_step,
    perturb_scale,
    step_seeds,
    hash_mults,
):
    bf16 = jnp.bfloat16
    f32 = jnp.float32
    feat_local = tokens.shape[1]
    unit_local = fc1_weight.shape[1]
    core = lax.axis_index("c")
    z_lo = lax.axis_index("zl")
    z_hi = lax.axis_index("zh")
    picks = [(core, CORE_SWAP)]
    for bits in STAGES:
        bit = jnp.where(core == 0, bits[0], bits[1])
        picks.append((lax.shift_right_logical(z_lo, bit) & 1, line_perm(bits)))

    values = tokens.astype(f32)
    row_mean = (total(jnp.sum(values, axis=1)) / D)[:, None]
    centered = values - row_mean
    row_var = (total(jnp.sum(centered * centered, axis=1)) / D)[:, None]
    normed = (
        centered * lax.rsqrt(row_var + 1e-05) * ln_gain.astype(f32) + ln_bias.astype(f32)
    ).astype(bf16)
    feat_ids = lax.axis_index(TENSOR) * feat_local + jnp.arange(feat_local, dtype=jnp.int32)
    unit_ids = lax.axis_index(FSDP) * unit_local + jnp.arange(unit_local, dtype=jnp.int32)
    first_index = feat_ids[:, None] * FF + unit_ids[None, :]
    plus_one, minus_one = new_weights(
        fc1_weight, first_index, update_step, perturb_scale, step_seeds, hash_mults
    )
    part = jnp.concatenate(
        [
            jnp.dot(normed, plus_one, preferred_element_type=f32).astype(bf16),
            jnp.dot(normed, minus_one, preferred_element_type=f32).astype(bf16),
        ],
        axis=1,
    )
    for which, perm in picks:
        other = lax.ppermute(half(part, 1 - which), TENSOR, perm)
        part = (half(part, which).astype(f32) + other.astype(f32)).astype(bf16)
    bias_one = fc1_bias.astype(f32)
    hidden = jax.nn.relu(part.astype(f32) + jnp.concatenate([bias_one, bias_one])).astype(bf16)
    for which, perm in picks[::-1]:
        hidden = join(hidden, lax.ppermute(hidden, TENSOR, perm), which)
    second_index = D * FF + unit_ids[:, None] * D + feat_ids[None, :]
    plus_two, minus_two = new_weights(
        fc2_weight, second_index, update_step, perturb_scale, step_seeds, hash_mults
    )
    out = jnp.concatenate(
        [
            jnp.dot(hidden[:, :unit_local], plus_two, preferred_element_type=f32),
            jnp.dot(hidden[:, unit_local:], minus_two, preferred_element_type=f32),
        ],
        axis=1,
    ).astype(bf16)
    width = 2 * feat_local
    out = out.reshape(4, 2, 4, -1, width).transpose(0, 2, 1, 3, 4).reshape(16, -1, width)
    out = lax.all_to_all(out, ("y", "x"), 0, 0, tiled=True)
    out = jnp.sum(out.astype(f32), axis=0)
    other = lax.ppermute(half(out, 1 - z_hi).astype(bf16), "zh", [(0, 1), (1, 0)])
    out = half(out, z_hi) + other.astype(f32)
    bias_two = fc2_bias.astype(f32)
    branch_plus = (out[:, :feat_local] + bias_two).astype(bf16)
    branch_minus = (out[:, feat_local:] + bias_two).astype(bf16)
    return (branch_plus, branch_minus)


def solution(mesh):
    fine = Mesh(mesh.devices.reshape(4, 2, 4, 8, 2), ("y", "zh", "x", "zl", "c"))
    in_specs = (
        P(None, TENSOR),
        P(TENSOR),
        P(TENSOR),
        P(TENSOR, FSDP),
        P(FSDP),
        P(FSDP, TENSOR),
        P(TENSOR),
        P(),
        P(),
        P(),
        P(),
    )
    out_specs = (P(FSDP, TENSOR), P(FSDP, TENSOR))
    return jax.shard_map(body, mesh=fine, in_specs=in_specs, out_specs=out_specs, check_vma=False)
```

```python
import jax
import jax.numpy as jnp
from jax import lax
from jax.sharding import Mesh, PartitionSpec as P

D = 9216
FF = 36864
TENSOR = ("zl", "c")
FSDP = ("y", "zh", "x")


def shift_xor(hashed, amount):
    return hashed ^ lax.shift_right_logical(hashed, jnp.int32(amount))


def hashed_noise(param_index, seed_value, hash_mults):
    mult_a = hash_mults[0] | 1
    mult_b = hash_mults[1] | 1
    mult_c = hash_mults[2] | 1
    hashed = param_index * mult_a + seed_value * mult_b
    hashed = shift_xor(hashed, 16)
    hashed = hashed * mult_c
    hashed = shift_xor(hashed, 13)
    hashed = hashed * mult_a
    hashed = shift_xor(hashed, 16)
    fraction = (hashed & 16777215).astype(jnp.float32) * (1.0 / 16777216.0)
    return (fraction - 0.5) * 3.4641016151377544


def new_weights(weight, param_index, update_step, perturb_scale, step_seeds, hash_mults):
    updated = (
        weight.astype(jnp.float32)
        - update_step[0] * hashed_noise(param_index, step_seeds[0], hash_mults)
    ).astype(jnp.bfloat16)
    updated = lax.optimization_barrier(updated)
    updated_f = updated.astype(jnp.float32)
    shift_term = perturb_scale[0] * hashed_noise(param_index, step_seeds[1], hash_mults)
    return (
        (updated_f + shift_term).astype(jnp.bfloat16),
        (updated_f - shift_term).astype(jnp.bfloat16),
    )


def line_perm(bit_of_core):
    return [(2 * z + c, 2 * (z ^ (1 << bit_of_core[c])) + c) for z in range(8) for c in range(2)]


STAGES = [(0, 1), (1, 0), (2, 2)]
CORE_SWAP = [(i, i ^ 1) for i in range(16)]


def half(array, which):
    rows = array.shape[0] // 2
    return lax.dynamic_slice_in_dim(array, which * rows, rows, 0)


def join(mine, other, which):
    return jnp.where(
        which == 0, jnp.concatenate([mine, other], 0), jnp.concatenate([other, mine], 0)
    )


def body(
    tokens,
    ln_gain,
    ln_bias,
    fc1_weight,
    fc1_bias,
    fc2_weight,
    fc2_bias,
    update_step,
    perturb_scale,
    step_seeds,
    hash_mults,
):
    bf16 = jnp.bfloat16
    f32 = jnp.float32
    feat_local = tokens.shape[1]
    unit_local = fc1_weight.shape[1]
    core = lax.axis_index("c")
    z_lo = lax.axis_index("zl")
    z_hi = lax.axis_index("zh")
    picks = [(core, CORE_SWAP)]
    for bits in STAGES:
        bit = jnp.where(core == 0, bits[0], bits[1])
        picks.append((lax.shift_right_logical(z_lo, bit) & 1, line_perm(bits)))

    values = tokens.astype(f32)
    local_mean = jnp.mean(values, axis=1)
    offset = values - local_mean[:, None]
    local_sq = jnp.sum(offset * offset, axis=1)
    stats = jnp.broadcast_to(jnp.stack([local_mean, local_sq])[None], (16, 2, tokens.shape[0]))
    stats = lax.all_to_all(stats, TENSOR, 0, 0, tiled=True)
    means = stats[:, 0]
    row_mean = jnp.mean(means, axis=0)
    spread = means - row_mean[None]
    row_var = (jnp.sum(stats[:, 1] + feat_local * spread * spread, axis=0) / D)[:, None]
    centered = values - row_mean[:, None]
    normed = (
        centered * lax.rsqrt(row_var + 1e-05) * ln_gain.astype(f32) + ln_bias.astype(f32)
    ).astype(bf16)
    feat_ids = lax.axis_index(TENSOR) * feat_local + jnp.arange(feat_local, dtype=jnp.int32)
    unit_ids = lax.axis_index(FSDP) * unit_local + jnp.arange(unit_local, dtype=jnp.int32)
    first_index = feat_ids[:, None] * FF + unit_ids[None, :]
    plus_one, minus_one = new_weights(
        fc1_weight, first_index, update_step, perturb_scale, step_seeds, hash_mults
    )
    plus_two, minus_two = new_weights(
        fc2_weight,
        D * FF + unit_ids[:, None] * D + feat_ids[None, :],
        update_step,
        perturb_scale,
        step_seeds,
        hash_mults,
    )
    bias_one = fc1_bias.astype(f32)
    bias_two = fc2_bias.astype(f32)
    hidden = []
    for weight in (plus_one, minus_one):
        part = jnp.dot(normed, weight, preferred_element_type=f32).astype(bf16)
        for which, perm in picks:
            other = lax.ppermute(half(part, 1 - which), TENSOR, perm)
            part = (half(part, which).astype(f32) + other.astype(f32)).astype(bf16)
        hidden.append(jax.nn.relu(part.astype(f32) + bias_one).astype(bf16))
    for stage in range(len(picks)):
        which, perm = picks[-1 - stage]
        hidden = [join(one, lax.ppermute(one, TENSOR, perm), which) for one in hidden]
    results = []
    for one, weight in zip(hidden, (plus_two, minus_two)):
        out = jnp.dot(one, weight, preferred_element_type=f32).astype(bf16)
        out = out.reshape(4, 2, 4, -1, feat_local).transpose(0, 2, 1, 3, 4)
        out = out.reshape(16, -1, feat_local)
        out = lax.all_to_all(out, ("y", "x"), 0, 0, tiled=True)
        out = jnp.sum(out.astype(f32), axis=0)
        other = lax.ppermute(half(out, 1 - z_hi).astype(bf16), "zh", [(0, 1), (1, 0)])
        results.append((half(out, z_hi) + other.astype(f32) + bias_two).astype(bf16))
    return tuple(results)


def solution(mesh):
    fine = Mesh(mesh.devices.reshape(4, 2, 4, 8, 2), ("y", "zh", "x", "zl", "c"))
    in_specs = (
        P(None, TENSOR),
        P(TENSOR),
        P(TENSOR),
        P(TENSOR, FSDP),
        P(FSDP),
        P(FSDP, TENSOR),
        P(TENSOR),
        P(),
        P(),
        P(),
        P(),
    )
    out_specs = (P(FSDP, TENSOR), P(FSDP, TENSOR))
    return jax.shard_map(body, mesh=fine, in_specs=in_specs, out_specs=out_specs, check_vma=False)
```

```python
import jax
import jax.numpy as jnp
from jax import lax
from jax.experimental import pallas as pl
from jax.experimental.pallas import tpu as pltpu
from jax.sharding import Mesh, PartitionSpec as P

D = 9216
FF = 36864
TENSOR = ("zl", "c")
FSDP = ("y", "zh", "x")


def shift_xor(hashed, amount):
    return hashed ^ lax.shift_right_logical(hashed, jnp.int32(amount))


def perturb_kernel(first, strides, block, strip, row_axes, col_axes):
    stride, col_stride = strides
    row_names, row_count = row_axes
    col_names, col_count = col_axes

    def kernel(seeds, mults, step, scale, weight, plus, minus):
        mult_a = mults[0] | 1
        mult_b = mults[1] | 1
        mult_c = mults[2] | 1
        unit = 3.4641016151377544 / 16777216.0
        step_unit = step[0] * unit
        scale_unit = scale[0] * unit
        columns = weight.shape[1]
        row_start = flat_index(row_names) * row_count + pl.program_id(0) * block
        start = first + row_start * stride + flat_index(col_names) * (col_count * col_stride)
        shape = (strip, columns)
        local = lax.broadcasted_iota(jnp.int32, shape, 0) * stride
        local = (local + lax.broadcasted_iota(jnp.int32, shape, 1) * col_stride) * mult_a

        def centred(hashed):
            hashed = shift_xor(hashed, 16)
            hashed = hashed * mult_c
            hashed = shift_xor(hashed, 13)
            hashed = hashed * mult_a
            hashed = shift_xor(hashed, 16)
            return ((hashed & 16777215) - 8388608).astype(jnp.float32)

        def body(index, carry):
            rows = pl.ds(index * strip, strip)
            base = (start + index * (strip * stride)) * mult_a
            noise = centred(local + (base + seeds[0] * mult_b))
            updated = (weight[rows, :].astype(jnp.float32) - step_unit * noise).astype(jnp.bfloat16)
            updated = updated.astype(jnp.float32)
            shift = scale_unit * centred(local + (base + seeds[1] * mult_b))
            plus[rows, :] = (updated + shift).astype(jnp.bfloat16)
            minus[rows, :] = (updated - shift).astype(jnp.bfloat16)
            return carry

        lax.fori_loop(0, block // strip, body, 0)

    return kernel


AXES = {"y": 4, "zh": 2, "x": 4, "zl": 8, "c": 2}


def flat_index(names):
    index = 0
    for name in names:
        index = index * AXES[name] + lax.axis_index(name)
    return index


def perturbed(weight, first, strides, row_names, col_names, scalars, steps):
    rows, columns = weight.shape
    block = rows // steps
    small = pl.BlockSpec(memory_space=pltpu.SMEM)
    tile = pl.BlockSpec((block, columns), lambda i: (i, 0))
    shape = jax.ShapeDtypeStruct((rows, columns), jnp.bfloat16)
    return pl.pallas_call(
        perturb_kernel(
            first, strides, block, 16, (row_names, rows), (col_names, columns)
        ),
        grid=(steps,),
        in_specs=[small] * 4 + [tile],
        out_specs=[tile, tile],
        out_shape=[shape, shape],
    )(*scalars, weight)


def line_perm(bit_of_core):
    return [(2 * z + c, 2 * (z ^ (1 << bit_of_core[c])) + c) for z in range(8) for c in range(2)]


STAGES = [(0, 1), (1, 0), (2, 2)]
CORE_SWAP = [(i, i ^ 1) for i in range(16)]


def after(value, earlier):
    return lax.optimization_barrier((value, earlier))[0]


def half(array, which):
    rows = array.shape[0] // 2
    return lax.dynamic_slice_in_dim(array, which * rows, rows, 0)


def join(mine, other, which):
    return jnp.where(
        which == 0, jnp.concatenate([mine, other], 0), jnp.concatenate([other, mine], 0)
    )


def body(
    tokens,
    ln_gain,
    ln_bias,
    fc1_weight,
    fc1_bias,
    fc2_weight,
    fc2_bias,
    update_step,
    perturb_scale,
    step_seeds,
    hash_mults,
):
    bf16 = jnp.bfloat16
    f32 = jnp.float32
    feat_local = tokens.shape[1]
    unit_local = fc1_weight.shape[1]
    core = lax.axis_index("c")
    z_lo = lax.axis_index("zl")
    z_hi = lax.axis_index("zh")
    picks = [(core, CORE_SWAP)]
    for bits in STAGES:
        bit = jnp.where(core == 0, bits[0], bits[1])
        picks.append((lax.shift_right_logical(z_lo, bit) & 1, line_perm(bits)))

    values = tokens.astype(f32)
    local_mean = jnp.mean(values, axis=1)
    offset = values - local_mean[:, None]
    local_sq = jnp.sum(offset * offset, axis=1)
    stats = jnp.broadcast_to(jnp.stack([local_mean, local_sq])[None], (16, 2, tokens.shape[0]))
    stats = lax.all_to_all(stats, TENSOR, 0, 0, tiled=True)
    scaled = (offset * ln_gain.astype(f32)).astype(bf16)
    slot = lax.broadcasted_iota(jnp.int32, (8, feat_local), 0)
    pair = jnp.where(slot == core, ln_gain[None], 0) + jnp.where(slot == 2, ln_bias[None], 0)
    pair = pair.astype(bf16)

    scalars = (step_seeds, hash_mults, update_step, perturb_scale)
    first_weights = perturbed(fc1_weight, 0, (FF, 1), TENSOR, FSDP, scalars, 4)
    second_weights = perturbed(fc2_weight.T, D * FF, (1, D), TENSOR, FSDP, scalars, 4)
    bias_one = fc1_bias.astype(f32)
    bias_two = fc2_bias.astype(f32)

    parts = [jnp.dot(scaled, w, preferred_element_type=f32).astype(bf16) for w in first_weights]
    sides = jnp.concatenate(
        [jnp.dot(pair, w, preferred_element_type=f32) for w in first_weights], axis=1
    )

    which, perm = picks[0]
    others = [lax.ppermute(half(part, 1 - which), TENSOR, perm) for part in parts]
    sides = sides + lax.ppermute(sides, TENSOR, perm)
    parts = [
        (half(part, which).astype(f32) + other.astype(f32)).astype(bf16)
        for part, other in zip(parts, others)
    ]

    which, perm = picks[1]
    rows = tokens.shape[0] // 4
    stats = lax.dynamic_slice_in_dim(stats, core * 2 * rows + which * rows, rows, 2)
    means = stats[:, 0]
    row_mean = jnp.mean(means, axis=0)
    spread = means - row_mean[None]
    row_var = jnp.sum(stats[:, 1] + feat_local * spread * spread, axis=0) / D
    row_scale = lax.rsqrt(row_var + 1e-05)[:, None]
    far = z_lo ^ jnp.where(core == 0, 1 << STAGES[0][0], 1 << STAGES[0][1])
    chips = lax.broadcasted_iota(jnp.int32, (16, rows), 0)
    near_rows = jnp.where(lax.shift_right_logical(chips, 1) == z_lo, spread, 0)
    far_rows = jnp.where(lax.shift_right_logical(chips, 1) == far, spread, 0)
    fold = lambda one: jnp.sum(one.reshape(8, 2, rows), axis=0)
    gap = jnp.zeros((6, rows), f32)
    spread = jnp.concatenate([fold(near_rows), gap, fold(far_rows), gap], axis=0)

    others = [lax.ppermute(half(part, 1 - which), TENSOR, perm) for part in parts]
    far_sides = lax.ppermute(sides, TENSOR, perm)
    both = jnp.concatenate([sides, far_sides], axis=0)
    shift = lax.dot_general(
        spread, both, (((0,), (0,)), ((), ())), precision=lax.Precision.HIGHEST
    )
    bias_sum = both[2:3] + both[10:11]
    for sign in range(2):
        columns = slice(sign * unit_local, (sign + 1) * unit_local)
        part = half(parts[sign], which).astype(f32) + others[sign].astype(f32)
        parts[sign] = (row_scale * (part + shift[:, columns]) + bias_sum[:, columns]).astype(bf16)

    hidden = []
    for part in parts:
        for which, perm in picks[2:]:
            other = lax.ppermute(half(part, 1 - which), TENSOR, perm)
            part = (half(part, which).astype(f32) + other.astype(f32)).astype(bf16)
        if hidden:
            part = after(part, hidden[0])
        hidden.append(jax.nn.relu(part.astype(f32) + bias_one).astype(bf16))
    for which, perm in picks[::-1]:
        hidden = [join(one, lax.ppermute(one, TENSOR, perm), which) for one in hidden]
    out = jnp.concatenate(
        [
            jnp.dot(one, weight.T, preferred_element_type=f32).astype(bf16)
            for one, weight in zip(hidden, second_weights)
        ],
        axis=1,
    )
    width = 2 * feat_local
    out = out.reshape(4, 2, 4, -1, width).transpose(0, 2, 1, 3, 4).reshape(16, -1, width)
    out = lax.all_to_all(out, ("y", "x"), 0, 0, tiled=True)
    out = jnp.sum(out.astype(f32), axis=0)
    other = lax.ppermute(half(out, 1 - z_hi).astype(bf16), "zh", [(0, 1), (1, 0)])
    out = half(out, z_hi) + other.astype(f32)
    branch_plus = (out[:, :feat_local] + bias_two).astype(bf16)
    branch_minus = (out[:, feat_local:] + bias_two).astype(bf16)
    return (branch_plus, branch_minus)


def solution(mesh):
    fine = Mesh(mesh.devices.reshape(4, 2, 4, 8, 2), ("y", "zh", "x", "zl", "c"))
    in_specs = (
        P(None, TENSOR),
        P(TENSOR),
        P(TENSOR),
        P(TENSOR, FSDP),
        P(FSDP),
        P(FSDP, TENSOR),
        P(TENSOR),
        P(),
        P(),
        P(),
        P(),
    )
    out_specs = (P(FSDP, TENSOR), P(FSDP, TENSOR))
    return jax.shard_map(body, mesh=fine, in_specs=in_specs, out_specs=out_specs, check_vma=False)
```

```python
import jax
import jax.numpy as jnp
from jax import lax
from jax.experimental import pallas as pl
from jax.experimental.pallas import tpu as pltpu
from jax.sharding import Mesh, PartitionSpec as P

D = 9216
FF = 36864
TENSOR = ("zl", "c")
FSDP = ("y", "zh", "x")


def shift_xor(hashed, amount):
    return hashed ^ lax.shift_right_logical(hashed, jnp.int32(amount))


def perturb_kernel(first, strides, block, strip, row_axes, col_axes):
    stride, col_stride = strides
    row_names, row_count = row_axes
    col_names, col_count = col_axes

    def kernel(seeds, mults, step, scale, weight, plus, minus):
        mult_a = mults[0] | 1
        mult_b = mults[1] | 1
        mult_c = mults[2] | 1
        unit = 3.4641016151377544 / 16777216.0
        step_unit = step[0] * unit
        scale_unit = scale[0] * unit
        columns = weight.shape[1]
        row_start = flat_index(row_names) * row_count + pl.program_id(0) * block
        start = first + row_start * stride + flat_index(col_names) * (col_count * col_stride)
        shape = (strip, columns)
        local = lax.broadcasted_iota(jnp.int32, shape, 0) * stride
        local = (local + lax.broadcasted_iota(jnp.int32, shape, 1) * col_stride) * mult_a

        def centred(hashed):
            hashed = shift_xor(hashed, 16)
            hashed = hashed * mult_c
            hashed = shift_xor(hashed, 13)
            hashed = hashed * mult_a
            hashed = shift_xor(hashed, 16)
            return ((hashed & 16777215) - 8388608).astype(jnp.float32)

        def body(index, carry):
            rows = pl.ds(index * strip, strip)
            base = (start + index * (strip * stride)) * mult_a
            noise = centred(local + (base + seeds[0] * mult_b))
            updated = (weight[rows, :].astype(jnp.float32) - step_unit * noise).astype(jnp.bfloat16)
            updated = updated.astype(jnp.float32)
            shift = scale_unit * centred(local + (base + seeds[1] * mult_b))
            plus[rows, :] = (updated + shift).astype(jnp.bfloat16)
            minus[rows, :] = (updated - shift).astype(jnp.bfloat16)
            return carry

        lax.fori_loop(0, block // strip, body, 0)

    return kernel


AXES = {"y": 4, "zh": 2, "x": 4, "zl": 8, "c": 2}


def flat_index(names):
    index = 0
    for name in names:
        index = index * AXES[name] + lax.axis_index(name)
    return index


def perturbed(weight, first, strides, row_names, col_names, scalars, steps):
    rows, columns = weight.shape
    block = rows // steps
    small = pl.BlockSpec(memory_space=pltpu.SMEM)
    tile = pl.BlockSpec((block, columns), lambda i: (i, 0))
    shape = jax.ShapeDtypeStruct((rows, columns), jnp.bfloat16)
    return pl.pallas_call(
        perturb_kernel(
            first, strides, block, 16, (row_names, rows), (col_names, columns)
        ),
        grid=(steps,),
        in_specs=[small] * 4 + [tile],
        out_specs=[tile, tile],
        out_shape=[shape, shape],
    )(*scalars, weight)


def line_perm(bit_of_core):
    return [(2 * z + c, 2 * (z ^ (1 << bit_of_core[c])) + c) for z in range(8) for c in range(2)]


STAGES = [(0, 1), (1, 0), (2, 2)]
STEPS = 7
TIES = {1: 2, 2: 3, 3: 4}
CORE_SWAP = [(i, i ^ 1) for i in range(16)]


def after(value, earlier):
    return lax.optimization_barrier((value, earlier))[0]


def half(array, which):
    rows = array.shape[0] // 2
    return lax.dynamic_slice_in_dim(array, which * rows, rows, 0)


def join(mine, other, which):
    return jnp.where(
        which == 0, jnp.concatenate([mine, other], 0), jnp.concatenate([other, mine], 0)
    )


def body(
    tokens,
    ln_gain,
    ln_bias,
    fc1_weight,
    fc1_bias,
    fc2_weight,
    fc2_bias,
    update_step,
    perturb_scale,
    step_seeds,
    hash_mults,
):
    bf16 = jnp.bfloat16
    f32 = jnp.float32
    feat_local = tokens.shape[1]
    unit_local = fc1_weight.shape[1]
    core = lax.axis_index("c")
    z_lo = lax.axis_index("zl")
    z_hi = lax.axis_index("zh")
    picks = [(core, CORE_SWAP)]
    for bits in STAGES:
        bit = jnp.where(core == 0, bits[0], bits[1])
        picks.append((lax.shift_right_logical(z_lo, bit) & 1, line_perm(bits)))

    values = tokens.astype(f32)
    local_mean = jnp.mean(values, axis=1)
    offset = values - local_mean[:, None]
    local_sq = jnp.sum(offset * offset, axis=1)
    stats = jnp.broadcast_to(jnp.stack([local_mean, local_sq])[None], (16, 2, tokens.shape[0]))
    stats = lax.all_to_all(stats, TENSOR, 0, 0, tiled=True)
    means = stats[:, 0]
    row_mean = jnp.mean(means, axis=0)
    spread = means - row_mean[None]
    row_var = (jnp.sum(stats[:, 1] + feat_local * spread * spread, axis=0) / D)[:, None]
    centered = values - row_mean[:, None]
    normed = (
        centered * lax.rsqrt(row_var + 1e-05) * ln_gain.astype(f32) + ln_bias.astype(f32)
    ).astype(bf16)
    normed = lax.optimization_barrier(normed)

    scalars = (step_seeds, hash_mults, update_step, perturb_scale)
    first_weights = perturbed(fc1_weight, 0, (FF, 1), TENSOR, FSDP, scalars, 4)
    bias_one = fc1_bias.astype(f32)
    bias_two = fc2_bias.astype(f32)

    def stream(sign):
        part = jnp.dot(normed, first_weights[sign], preferred_element_type=f32).astype(bf16)
        for which, perm in picks[:3]:
            send = yield half(part, 1 - which)
            other = lax.ppermute(send, TENSOR, perm)
            part = (half(part, which).astype(f32) + other.astype(f32)).astype(bf16)
        part = yield part
        other = lax.ppermute(part, TENSOR, picks[3][1])
        part = jax.nn.relu(part.astype(f32) + other.astype(f32) + bias_one).astype(bf16)
        for which, perm in picks[2::-1]:
            part = yield part
            part = join(part, lax.ppermute(part, TENSOR, perm), which)
        out = jnp.dot(part, second_weights[sign].T, preferred_element_type=f32).astype(bf16)
        yield out

    def scatter(out):
        out = lax.all_to_all(out, ("y", "x"), 0, 0, tiled=True)
        return jnp.sum(out.astype(f32), axis=0)

    plus = stream(0)
    minus = stream(1)
    ahead = [next(plus)]
    behind = next(minus)
    second_weights = []
    for step in range(STEPS):
        if step == 4:
            held = after(fc2_weight.T, ahead[step])
            second_weights += perturbed(held, D * FF, (1, D), TENSOR, FSDP, scalars, 4)
        if step == 6:
            ahead[step] = after(ahead[step], second_weights[0])
        ahead.append(plus.send(ahead[-1]))
    for step in range(STEPS):
        if step in TIES:
            behind = after(behind, ahead[TIES[step]])
        behind = minus.send(behind)
    out = scatter(blocks(jnp.concatenate([ahead[-1], behind], axis=1)))
    other = lax.ppermute(half(out, 1 - z_hi).astype(bf16), "zh", [(0, 1), (1, 0)])
    out = half(out, z_hi) + other.astype(f32)
    branch_plus = (out[:, :feat_local] + bias_two).astype(bf16)
    branch_minus = (out[:, feat_local:] + bias_two).astype(bf16)
    return (branch_plus, branch_minus)


def blocks(out):
    out = out.reshape(4, 2, 4, -1, out.shape[1]).transpose(0, 2, 1, 3, 4)
    return out.reshape(16, -1, out.shape[-1])


def solution(mesh):
    fine = Mesh(mesh.devices.reshape(4, 2, 4, 8, 2), ("y", "zh", "x", "zl", "c"))
    in_specs = (
        P(None, TENSOR),
        P(TENSOR),
        P(TENSOR),
        P(TENSOR, FSDP),
        P(FSDP),
        P(FSDP, TENSOR),
        P(TENSOR),
        P(),
        P(),
        P(),
        P(),
    )
    out_specs = (P(FSDP, TENSOR), P(FSDP, TENSOR))
    return jax.shard_map(body, mesh=fine, in_specs=in_specs, out_specs=out_specs, check_vma=False)
```
